32 devices in a mesh: pipe: 2 (over x), expert: 16 (over z, y, core).
Axes of the slice: x: 2, y: 2, z: 4, core: 2. Of those that a mesh axis runs over, the one named last changes fastest.
Arguments:
- inputs: bfloat16 [1, 512, 5120], P(None, 'expert'), may hold values from -6 to 6
- router: bfloat16 [2, 5120, 2], P('pipe'), may hold values from -0.078125 to 0.078125
- w_up: bfloat16 [2, 3072, 5120], P('pipe', 'expert'), may hold values from -0.078125 to 0.078125
- w_down: bfloat16 [2, 3072, 5120], P('pipe', 'expert'), may hold values from -0.15625 to 0.15625
- picks: int32 [2, 1, 2, 8], P('pipe'), may hold values from 0 to 511, as said below
- probe: bfloat16 [2, 64, 5120], P('pipe'), may hold values from -0.078125 to 0.078125
Outputs:
- student_feats: bfloat16 [2, 1, 512, 64], P('pipe', None, 'expert')
The draws below stay inside these ranges and needn't reach their ends.
Inputs may be any that keep to these rules, and one draw needn't show every extreme that they name: Each list picks[s, m, e] holds 8 different token positions of the micro-batch. Of the 32 consecutive positions held by one index of expert, at most 1 stand in one list, and in every list some index has exactly 1.
All inputs are finite; a program needn't handle non-finite values.
Results may differ from the reference program's by a relative error of at most 0.0059.
Values may be sent and summed in bfloat16 or wider, within the bound.
A program may use at most 64 MiB of HBM per device.

```python
import jax
import jax.numpy as jnp
from jax import lax

D = 5120
EXPERT_FF = 1536
SPLIT = 8
SLOT = 1
PROJ = 64
TOK_DEV = 32
MICRO = 1
FF_DEV = 192
EXPERTS = 2
SECTIONS = 2
TOKENS = 512
CAP = 8


def draw_picks(key, part):
    sources = TOKENS // TOK_DEV
    tickets = sources * SLOT
    list_count = SECTIONS * MICRO * EXPERTS

    def offset_order(offset_key):
        return jax.random.permutation(offset_key, TOK_DEV)

    def one_list(list_key):
        order_key, first_key, offset_key = jax.random.split(list_key, 3)
        shuffled = jax.random.permutation(order_key, tickets).astype(jnp.int32)
        leading = jax.random.randint(first_key, (), 0, sources).astype(jnp.int32)
        ranks = jnp.arange(tickets, dtype=jnp.int32)
        scores = jnp.where(shuffled // SLOT == leading, ranks - tickets, ranks)
        chosen = shuffled[jnp.argsort(scores)][:CAP]
        offsets = jax.vmap(offset_order)(jax.random.split(offset_key, sources)).astype(jnp.int32)
        owners = chosen // SLOT
        return (owners * TOK_DEV + offsets[owners, chosen % SLOT]).astype(jnp.int32)
    picked = jax.vmap(one_list)(jax.random.split(key, list_count))
    return picked.reshape(SECTIONS, MICRO, EXPERTS, CAP)


def block_scale(key, extent, pieces, smallest, high):
    def one(dim, parts):
        steps = jax.random.uniform(jax.random.fold_in(jax.random.fold_in(key, 6), dim), (parts,), jnp.float32, smallest / len(pieces), high / len(pieces))
        return jnp.repeat(jnp.exp(steps), extent[dim] // parts).reshape((-1,) + (1,) * (len(extent) - dim - 1))

    loudness = one(*pieces[0])
    for cut in pieces[1:]:
        loudness = loudness * one(*cut)
    return loudness


def centred(rng, extent, width, limit, cuts=(), kind=jnp.bfloat16):
    gain = block_scale(rng, extent, cuts, -0.22, 0.18) if cuts else 1.0
    entries = jax.random.normal(rng, extent, jnp.float32) * width * gain
    return jnp.minimum(jnp.maximum(entries, -limit), limit).astype(kind)


def setup_inputs(seed: int = 0) -> dict:
    key_of = jax.random.split(jax.random.key(seed), 7)
    return {
        "inputs": centred(key_of[0], (MICRO, TOKENS, D), 1.0, 6.0, ((1, 16),)),
        "router": centred(key_of[1], (SECTIONS, D, EXPERTS), D ** -0.5, 0.078125, ((0, 2),)),
        "w_up": centred(key_of[2], (SECTIONS, EXPERTS * EXPERT_FF, D), D ** -0.5, 0.078125, ((0, 2), (1, 16))),
        "w_down": centred(key_of[3], (SECTIONS, EXPERTS * EXPERT_FF, D), EXPERT_FF ** -0.5, 0.15625, ((0, 2), (1, 16))),
        "picks": draw_picks(jax.random.fold_in(key_of[6], 71), 0),
        "probe": centred(key_of[5], (SECTIONS, PROJ, D), D ** -0.5, 0.078125, ((0, 2),)),
    }


def rms_rows(rows_in):
    wide = rows_in.astype(jnp.float32)
    scale = lax.rsqrt(lax.optimization_barrier(jnp.mean(wide * wide, axis=-1, keepdims=True)) + 1e-06)
    return (wide * scale).astype(jnp.bfloat16)

def section_step(rows_in, router_s, up_s, down_s, picks_sm):
    normed = rms_rows(rows_in)
    gate_values = jax.nn.sigmoid(jnp.dot(normed, router_s, preferred_element_type=jnp.float32))

    def one_expert(update, expert):
        chosen = picks_sm[expert]
        chosen_rows = jnp.take(normed, chosen, axis=0)
        up_block = lax.dynamic_slice_in_dim(up_s, expert * EXPERT_FF, EXPERT_FF, 0)
        down_block = lax.dynamic_slice_in_dim(down_s, expert * EXPERT_FF, EXPERT_FF, 0)
        pre = lax.dot_general(chosen_rows, up_block, (((1,), (1,)), ((), ())), preferred_element_type=jnp.float32)
        hidden = jax.nn.silu(pre).astype(jnp.bfloat16)
        blocks = jnp.einsum('cki,kid->kcd', hidden.reshape(CAP, SPLIT, FF_DEV).astype(jnp.float32), down_block.reshape(SPLIT, FF_DEV, D).astype(jnp.float32))
        blocks = lax.optimization_barrier(blocks.astype(jnp.bfloat16))
        expert_out = lax.optimization_barrier(jnp.sum(blocks.astype(jnp.float32), axis=0))
        gate_rows = gate_values[chosen, expert]
        update = update.at[chosen].add(gate_rows[:, None] * expert_out)
        return (update, None)
    update, _ = lax.scan(one_expert, jnp.zeros((TOKENS, D), jnp.float32), jnp.arange(EXPERTS, dtype=jnp.int32))
    return (rows_in.astype(jnp.float32) + update).astype(jnp.bfloat16)

def reference(inputs, router, w_up, w_down, picks, probe):
    finals = []
    for micro_index in range(MICRO):
        hidden_rows = inputs[micro_index]
        for section_index in range(SECTIONS):
            hidden_rows = section_step(hidden_rows, router[section_index], w_up[section_index], w_down[section_index], picks[section_index, micro_index])
        finals.append(hidden_rows)
    final = jnp.stack(finals)
    final_normed = rms_rows(final)
    student_rows = jnp.einsum('mtd,pjd->pmtj', final_normed.astype(jnp.float32), probe.astype(jnp.float32))
    return student_rows.astype(jnp.bfloat16)
```

```python
import functools

import jax
import jax.numpy as jnp
from jax import lax
from jax.experimental import pallas as pl
from jax.experimental.pallas import tpu as pltpu
from jax.sharding import PartitionSpec as P

EPS = 1e-06
CUT = 8
PAD = 16
JOIN = 2
LANE = 128
BLOCK = 8
MESH = pl.DeviceIdType.MESH
NT = (((1,), (1,)), ((), ()))


class Plan:
    def __init__(self, sections, width, features):
        self.piece = features // CUT
        tiles = self.piece // LANE
        self.per = width // CUT
        self.parts = min(self.per, tiles, sections)
        sizes = [tiles // self.parts + (q < tiles % self.parts) for q in range(self.parts)]
        starts = [sum(sizes[:q]) for q in range(self.parts)]
        self.window = max(sizes) * LANE
        self.size = [size * LANE for size in sizes]
        self.start = [start * LANE for start in starts]
        self.win = [min(start, self.piece - self.window) for start in self.start]
        self.off = [start - win for start, win in zip(self.start, self.win)]


def kernel(
    sections, width, experts, plan, x_hbm, router_hbm, up_hbm, down_hbm, picks_hbm, probe_hbm,
    out_ref, x_ref, up_ref, down_ref, probe_ref, scorer, lists, columns, place, picked, arrived,
    stage, listed, xrows, xin, base_rows, pin, state_out, state_in, sent, fed, owed, owing, held,
    partial, returned, done_out, done_in, load_sem, list_send, list_recv, row_send, row_recv,
    x_send, x_recv, pin_send, pin_recv, state_send, state_recv, fed_send, fed_recv, owe_send,
    owe_recv, part_send, part_recv, done_send, done_recv,
):
    section = lax.axis_index("pipe")
    me = lax.axis_index("expert")
    tokens, features = x_ref.shape
    hidden_units = up_hbm.shape[0]
    cap = lists.shape[2]
    piece, per, parts, window = plan.piece, plan.per, plan.parts, plan.window
    group = width // experts
    slots = sections * experts
    blocks, filled = xin.shape[1], min(slots, BLOCK)
    last = sections - 1
    expert = me // group
    my_cut = me // per
    my_part = lax.rem(me, per)
    barrier = pltpu.get_barrier_semaphore()

    def far_pipe(far):
        index = section + far
        return jnp.where(index >= sections, index - sections, index)

    def each_other(act):
        if width <= 16:
            for step in reversed(range(1, width)):
                act(jnp.bitwise_xor(me, step))
        else:
            lax.fori_loop(
                1, width, lambda step, carry: (act(jnp.bitwise_xor(me, width - step)), carry)[1], 0
            )

    def if_slicing(act):
        if per == parts:
            act()
        else:
            pl.when(my_part < parts)(act)

    def remote(src, dst, send, recv, to):
        return pltpu.make_async_remote_copy(
            src_ref=src, dst_ref=dst, send_sem=send, recv_sem=recv, device_id=to,
            device_id_type=MESH,
        )

    def wait(ref, sem):
        pltpu.make_async_copy(ref, ref, sem).wait()

    def greet(other):
        for far in range(sections):
            pl.semaphore_signal(
                barrier, inc=1, device_id=(far_pipe(far), other), device_id_type=MESH
            )

    for far in range(1, sections):
        pl.semaphore_signal(barrier, inc=1, device_id=(far_pipe(far), me), device_id_type=MESH)
    each_other(greet)

    loads = [
        pltpu.make_async_copy(picks_hbm, lists.at[section], load_sem.at[0]),
        pltpu.make_async_copy(x_hbm, x_ref, load_sem.at[1]),
        pltpu.make_async_copy(up_hbm, up_ref.at[pl.ds(0, hidden_units)], load_sem.at[2]),
        pltpu.make_async_copy(router_hbm, scorer, load_sem.at[3]),
        pltpu.make_async_copy(down_hbm, down_ref, load_sem.at[4]),
        pltpu.make_async_copy(probe_hbm, probe_ref, load_sem.at[5]),
    ]
    for load in loads:
        load.start()
    loads[0].wait()
    loads[1].wait()

    def places_of(section_lists):
        wide = jnp.concatenate(
            [jnp.broadcast_to(section_lists[e : e + 1], (CUT, section_lists.shape[1]))
             for e in range(experts)], axis=0,
        )
        local = wide - me * tokens
        owned = (local >= 0) & (local < tokens)
        found = jnp.where(owned, local + 1, 0).astype(jnp.float32)
        return jnp.sum(found, axis=1, keepdims=True) - 1.0

    def select(places):
        height = experts * CUT
        token_id = lax.broadcasted_iota(jnp.int32, (height, tokens), 1).astype(jnp.float32)
        cut_id = lax.rem(lax.broadcasted_iota(jnp.int32, (height, tokens), 0), CUT)
        hot = places == token_id
        total = jnp.zeros((height, piece), jnp.float32)
        for c in range(CUT):
            pick = jnp.where(hot & (cut_id == c), 1.0, 0.0).astype(jnp.bfloat16)
            total += jnp.dot(
                pick, x_ref[:, c * piece : (c + 1) * piece], preferred_element_type=jnp.float32
            )
        return total

    def note(which):
        section_lists = lists[which]
        places = places_of(section_lists)
        place[pl.ds(which * experts, experts)] = jnp.broadcast_to(
            places, (experts * CUT, LANE)
        ).reshape(experts, CUT, LANE)
        diagonal = lax.broadcasted_iota(jnp.int32, (cap, cap), 0) == lax.broadcasted_iota(
            jnp.int32, (cap, cap), 1
        )
        for e in range(experts):
            wide = jnp.broadcast_to(section_lists[e : e + 1], (cap, cap)).astype(jnp.float32)
            column = jnp.sum(jnp.where(diagonal, wide, 0.0), axis=1, keepdims=True)
            columns[which * experts + e] = jnp.broadcast_to(column, columns.shape[1:])
        return places

    places = note(section)

    @pl.when(section == 0)
    def _():
        picked[...] = select(places).astype(jnp.bfloat16).reshape(experts, CUT, piece)

    pl.semaphore_wait(barrier, sections * width - 1)

    def expert_of(index):
        owner = jnp.int32(0)
        for e in range(1, experts):
            owner = owner + (index >= e * group).astype(jnp.int32)
        return owner

    @pl.when(section == 0)
    def _():
        each_other(
            lambda other: remote(
                picked.at[expert_of(other)], arrived.at[me], row_send, row_recv, (section, other)
            ).start()
        )
        pltpu.make_async_copy(picked.at[expert], arrived.at[me], row_recv).start()

    def list_copy(far):
        return remote(
            lists.at[section], lists.at[section], list_send.at[far], list_recv.at[far],
            (far_pipe(far), me),
        )

    for far in range(1, sections):
        list_copy(far).start()
    for far in range(1, sections):
        list_copy(far).wait()
        note(lax.rem(section + sections - far, sections))

    def each_slice(act):
        for step in reversed(range(CUT)):
            cut = jnp.bitwise_xor(my_cut, step)
            for q in range(parts):
                act(step, cut, q, cut * per + q)

    def owner_lanes(height_rows, first_block):
        rows_n, lanes_n = filled * cap, width * BLOCK
        row_slot = lax.broadcasted_iota(jnp.int32, (rows_n, lanes_n), 0) // cap
        lane = lax.broadcasted_iota(jnp.int32, (rows_n, lanes_n), 1)
        low = (lane // BLOCK * tokens).astype(jnp.float32)
        return (row_slot == lane % BLOCK) & (height_rows >= low) & (height_rows < low + tokens)

    def column_of(block):
        wide = columns[pl.ds(block * filled, filled)]
        return wide.reshape(filled * cap, wide.shape[2])[:, :1]

    def row_of(column):
        count = column.shape[0]
        diagonal = lax.broadcasted_iota(jnp.int32, (count, count), 0) == lax.broadcasted_iota(
            jnp.int32, (count, count), 1
        )
        wide = jnp.where(diagonal, jnp.broadcast_to(column, (count, count)), 0.0)
        return jnp.sum(wide, axis=0, keepdims=True)

    @pl.when(section == 1)
    def _():
        token_id = lax.broadcasted_iota(jnp.int32, (BLOCK, tokens), 1).astype(jnp.float32)
        row_id = lax.broadcasted_iota(jnp.int32, (BLOCK, tokens), 0)
        for b in range(blocks):
            hot = jnp.zeros((BLOCK, tokens), jnp.float32)
            for i in range(filled):
                at = place[b * filled + i][:1, :1]
                hot = jnp.where((row_id == i) & (at == token_id), 1.0, hot)
            for c in range(CUT):
                xrows[c, b] = jnp.dot(
                    hot.astype(jnp.bfloat16), x_ref[:, c * piece : (c + 1) * piece],
                    preferred_element_type=jnp.float32,
                ).astype(jnp.bfloat16)

        def send(step, cut, q, device):
            src = xrows.at[cut, :, :, pl.ds(plan.win[q], window)]

            def away():
                remote(src, xin.at[me], x_send, x_recv, (section, device)).start()

            if step:
                away()
            else:
                pl.when(device != me)(away)

                @pl.when(device == me)
                def _():
                    pltpu.make_async_copy(src, xin.at[me], x_recv).start()

        each_slice(send)

    loads[5].wait()
    x_all = x_ref[...]
    raw = lax.dot_general(x_all, probe_ref[...], NT, preferred_element_type=jnp.float32)
    x_wide = x_all.astype(jnp.float32)
    square = jnp.sum(x_wide * x_wide, axis=1, keepdims=True)
    base = raw * lax.rsqrt(square * (1.0 / features) + EPS)

    loads[2].wait()
    loads[3].wait()
    up_ref[pl.ds(hidden_units, PAD)] = jnp.zeros((PAD, features), jnp.bfloat16)
    up_ref[pl.ds(hidden_units, experts)] = scorer[...]
    loads[4].wait()

    @pl.when(section == 1)
    def _():
        def gather():
            wait(xin, x_recv)
            for b in range(blocks):
                rows = xin[:, b].astype(jnp.float32).reshape(width * BLOCK, window)
                hot = owner_lanes(column_of(b), b).astype(jnp.float32).astype(jnp.bfloat16)
                total = jnp.dot(hot, rows.astype(jnp.bfloat16), preferred_element_type=jnp.float32)
                base_rows[pl.ds(b * filled, filled)] = total.reshape(filled, cap, window)

        if_slicing(gather)

    def hidden_of(pre, squares):
        scale = lax.rsqrt(squares * (1.0 / features) + EPS)
        pre = pre * scale
        column = lax.broadcasted_iota(jnp.int32, pre.shape, 1)
        logit = jnp.sum(
            jnp.where(column == hidden_units + expert, pre, 0.0), axis=1, keepdims=True
        )
        value = pre[:, :hidden_units]
        gate = 1.0 / (1.0 + jnp.exp(-logit))
        return (value / (1.0 + jnp.exp(-value)) * gate).astype(jnp.bfloat16)

    def first_hidden():
        wait(arrived, row_recv)
        wide = arrived[...].astype(jnp.float32).reshape(width * CUT, piece)
        for t in range(piece // LANE):
            stage[t] = wide[:, t * LANE : (t + 1) * LANE]
        squares = jnp.sum((wide * wide).reshape(width, CUT, piece), axis=1)
        pre = jnp.zeros((width, up_ref.shape[0]), jnp.float32)
        for c in range(0, CUT, JOIN):
            pre += lax.dot_general(
                jnp.concatenate(
                    [stage[t, pl.ds(c + i, width, stride=CUT)]
                     for i in range(JOIN) for t in range(piece // LANE)], axis=1
                ).astype(jnp.bfloat16),
                up_ref[:, c * piece : (c + JOIN) * piece], NT,
                preferred_element_type=jnp.float32,
            )
        hidden = hidden_of(pre, jnp.sum(squares, axis=1, keepdims=True))
        column = columns[section * experts + expert][:, :1]
        low = (lax.broadcasted_iota(jnp.int32, (cap, width), 1) * tokens).astype(jnp.float32)
        hot = jnp.where((column >= low) & (column < low + tokens), 1.0, 0.0).astype(jnp.bfloat16)
        return jnp.dot(hot, hidden, preferred_element_type=jnp.float32).astype(jnp.bfloat16)

    def next_hidden():
        pre = jnp.zeros((cap, up_ref.shape[0]), jnp.float32)
        squares = jnp.zeros((cap, piece), jnp.float32)
        for step in range(CUT):
            cut = jnp.bitwise_xor(my_cut, step)
            for q in range(parts):
                wait(fed.at[cut * per + q], fed_recv.at[cut * per + q])
            chunk = jnp.concatenate(
                [fed[cut * per + q][:, plan.off[q] : plan.off[q] + plan.size[q]]
                 for q in range(parts)], axis=1,
            )
            wide = chunk.astype(jnp.float32)
            squares += wide * wide
            pre += lax.dot_general(
                chunk, up_ref[:, pl.ds(pl.multiple_of(cut * piece, LANE), piece)], NT,
                preferred_element_type=jnp.float32,
            )
        return hidden_of(pre, jnp.sum(squares, axis=1, keepdims=True))

    def pass_lists(hidden):
        def send(step, cut, q, device):
            if q == 0:
                listed[cut] = jnp.dot(
                    hidden, down_ref[:, pl.ds(pl.multiple_of(cut * piece, LANE), piece)],
                    preferred_element_type=jnp.float32,
                ).astype(jnp.bfloat16)
            remote(
                listed.at[cut, :, pl.ds(plan.win[q], window)], pin.at[me], pin_send, pin_recv,
                (section + 1, device),
            ).start()

        each_slice(send)

    def share_parts(hidden):
        own_list = jnp.zeros((1, cap), jnp.int32)
        for e in range(experts):
            own_list = jnp.where(expert == e, lists[section][e : e + 1], own_list)
        low = lax.broadcasted_iota(jnp.int32, (width, cap), 0) * tokens
        hot = (own_list >= low) & (own_list < low + tokens)
        hidden = jnp.dot(
            jnp.where(hot, 1.0, 0.0).astype(jnp.bfloat16), hidden,
            preferred_element_type=jnp.float32,
        ).astype(jnp.bfloat16)
        for c in range(0, CUT, JOIN):
            block = jnp.dot(
                hidden, down_ref[:, c * piece : (c + JOIN) * piece],
                preferred_element_type=jnp.float32,
            )
            for i in range(JOIN):
                for t in range(piece // LANE):
                    at = i * piece + t * LANE
                    stage[t, pl.ds(c + i, width, stride=CUT)] = block[:, at : at + LANE]
        for t in range(piece // LANE):
            partial[:, :, t * LANE : (t + 1) * LANE] = (
                stage[t].reshape(width, CUT, LANE).astype(jnp.bfloat16)
            )

        def refs(owner, q):
            return (
                partial.at[owner, :, pl.ds(plan.start[q], plan.size[q])],
                returned.at[me, :, pl.ds(plan.off[q], plan.size[q])],
            )

        def give(owner, q):
            src, dst = refs(owner, q)
            remote(src, dst, part_send.at[q], part_recv, (section - q, owner)).start()

        for q in reversed(range(1, parts)):
            give(me, q)

        def give_all(owner):
            for q in reversed(range(parts)):
                give(owner, q)

        each_other(give_all)
        src, dst = refs(me, 0)
        pltpu.make_async_copy(src, dst, part_recv).start()

    def state_copy():
        return remote(state_out, state_in, state_send, state_recv, (section + 1, me))

    def take_lists(last_section):
        if sections > 2:
            @pl.when(section > 1)
            def _():
                wait(state_in, state_recv)
                base_rows[...] = state_in[...].astype(jnp.float32)

        wait(pin, pin_recv)
        sums = jnp.concatenate(
            [jnp.sum(pin[pl.ds(e * group, group)].astype(jnp.float32), axis=0)
             for e in range(experts)], axis=0,
        )
        high = sums.astype(jnp.bfloat16)
        low = (sums - high.astype(jnp.float32)).astype(jnp.bfloat16)
        before = columns[pl.ds((section - 1) * experts, experts)]
        entries = row_of(before.reshape(experts * cap, before.shape[2])[:, :1])

        def grow(first, count):
            wide = columns[pl.ds(first, count)]
            same = wide.reshape(count * cap, wide.shape[2])[:, :1] == entries
            hot = jnp.where(same, 1.0, 0.0).astype(jnp.bfloat16)
            added = jnp.dot(hot, high, preferred_element_type=jnp.float32) + jnp.dot(
                hot, low, preferred_element_type=jnp.float32
            )
            rows = base_rows[pl.ds(first, count)] + added.reshape(count, cap, window)
            return rows.astype(jnp.bfloat16)

        sent[...] = grow(section * experts, experts)
        each_other(
            lambda other: remote(
                sent.at[expert_of(other)], fed.at[me], fed_send, fed_recv.at[me], (section, other)
            ).start()
        )
        pltpu.make_async_copy(sent.at[expert], fed.at[me], fed_recv.at[me]).start()
        for b in range(blocks):
            rows = grow(b * filled, filled)
            if sections > 2:
                state_out[pl.ds(b * filled, filled)] = rows
            owed_block(b, rows.reshape(filled * cap, window))
        if sections > 2:
            pl.when(section < last)(lambda: state_copy().start())
        pl.when(section == last)(owe)

    def owed_block(b, rows):
        @pl.when(section == last)
        def _():
            rows_n, lanes_n = width * BLOCK, filled * cap
            entry = row_of(column_of(b))
            row = lax.broadcasted_iota(jnp.int32, (rows_n, lanes_n), 0)
            lane_slot = lax.broadcasted_iota(jnp.int32, (rows_n, lanes_n), 1) // cap
            low = (row // BLOCK * tokens).astype(jnp.float32)
            hot = (row % BLOCK == lane_slot) & (entry >= low) & (entry < low + tokens)
            total = jnp.dot(
                jnp.where(hot, 1.0, 0.0).astype(jnp.bfloat16), rows,
                preferred_element_type=jnp.float32,
            )
            owed[:, b] = total.reshape(width, BLOCK, window).astype(jnp.bfloat16)

    def owe():
        def send(owner):
            remote(
                owed.at[owner], owing.at[my_cut], owe_send, owe_recv, (last - my_part, owner)
            ).start()

        each_other(send)
        pl.when(my_part > 0)(lambda: send(me))

        @pl.when(my_part == 0)
        def _():
            pltpu.make_async_copy(owed.at[me], owing.at[my_cut], owe_recv).start()

    @pl.when(section == 0)
    def _():
        pass_lists(first_hidden())

    if sections > 2:
        @pl.when((section > 0) & (section < last))
        def _():
            if_slicing(lambda: take_lists(False))
            pass_lists(next_hidden())

    @pl.when(section == last)
    def _():
        if_slicing(lambda: take_lists(True))
        share_parts(next_hidden())

    def done_copy(far):
        mine = last - section
        return remote(
            done_out, done_in.at[mine], done_send.at[far], done_recv.at[mine],
            (far_pipe(far), me),
        )

    def finish(q):
        wait(owing, owe_recv)
        for c in range(CUT):
            for b in range(blocks):
                rows = owing[c, b].astype(jnp.float32)
                for t in range(window // LANE):
                    held[t, pl.ds(b * filled * CUT + c, filled, stride=CUT)] = rows[
                        :filled, t * LANE : (t + 1) * LANE
                    ]
        span = returned.at[:, :, pl.ds(plan.off[q], plan.size[q])]
        wait(span, part_recv)
        lanes = slice(plan.off[q], plan.off[q] + plan.size[q])
        updates = [
            jnp.sum(returned[pl.ds(e * group, group), :, lanes].astype(jnp.float32), axis=0)
            for e in range(experts)
        ]
        for slot in range(slots):
            for t in range(plan.size[q] // LANE):
                tile = plan.off[q] // LANE + t
                rows = held[tile, pl.ds(slot * CUT, CUT)]
                for e in range(experts):
                    same = place[slot] == place[last * experts + e]
                    rows += jnp.where(same, updates[e][:, t * LANE : (t + 1) * LANE], 0.0)
                done_out[slot, :, tile * LANE : (tile + 1) * LANE] = rows.astype(jnp.bfloat16)
        for far in range(1, sections):
            remote(
                done_out.at[:, :, pl.ds(plan.off[q], plan.size[q])],
                done_in.at[q, :, :, pl.ds(plan.off[q], plan.size[q])],
                done_send.at[far], done_recv.at[q], (far_pipe(far), me),
            ).start()

        done_in[q, :, :, lanes] = done_out[:, :, lanes]

    for q in range(parts):
        pl.when(section == last - q)(functools.partial(finish, q))

    for q in range(parts):
        @pl.when(section != last - q)
        def _():
            wait(done_in.at[q, :, :, pl.ds(plan.off[q], plan.size[q])], done_recv.at[q])

    def over_cuts(value):
        count, lanes = value.shape
        summed = jnp.sum(value.reshape(count // CUT, CUT, lanes), axis=1, keepdims=True)
        return jnp.broadcast_to(summed, (count // CUT, CUT, lanes)).reshape(count, lanes)

    height = slots * CUT
    wide = jnp.concatenate(
        [done_in[q][:, :, plan.off[q] : plan.off[q] + plan.size[q]].astype(jnp.float32)
         for q in range(parts)], axis=2,
    ).reshape(height, piece)
    mean = over_cuts(jnp.sum(wide * wide, axis=1, keepdims=True)) * (1.0 / features)
    narrow = wide.astype(jnp.bfloat16)
    feats = probe_ref.shape[0]
    cut_out = lax.rem(lax.broadcasted_iota(jnp.int32, (height, feats), 0), CUT)
    changed = jnp.zeros((height, feats), jnp.float32)
    for c in range(CUT):
        term = lax.dot_general(
            narrow, probe_ref[:, c * piece : (c + 1) * piece], NT,
            preferred_element_type=jnp.float32,
        )
        changed = jnp.where(cut_out == c, term, changed)
    changed = over_cuts(changed) * lax.rsqrt(mean + EPS)
    token_id = lax.broadcasted_iota(jnp.int32, (tokens, feats), 0).astype(jnp.float32)
    result = base
    for slot in range(slots):
        at = place[slot][:1, :feats]
        result = jnp.where(token_id == at, changed[slot * CUT : slot * CUT + 1], result)
    out_ref[...] = result.astype(out_ref.dtype)

    @pl.when(section == 0)
    def _():
        most = arrived.at[pl.ds(0, width - 1)]
        wait(most, row_send)

    @pl.when(section < last)
    def _():
        for _ in range(1):
            whole = pin.at[pl.ds(0, CUT * parts)]
            wait(whole, pin_send)
        if sections > 2:
            @pl.when(section > 0)
            def _():
                if_slicing(lambda: wait(state_out, state_send))

    @pl.when(section == 1)
    def _():
        slices = CUT * parts
        if per == parts:
            wait(xin.at[pl.ds(0, slices - 1)], x_send)
        else:
            pl.when(my_part < parts)(lambda: wait(xin.at[pl.ds(0, slices - 1)], x_send))
            pl.when(my_part >= parts)(lambda: wait(xin.at[pl.ds(0, slices)], x_send))

    @pl.when(section > 0)
    def _():
        if_slicing(lambda: wait(fed.at[pl.ds(0, width - 1)], fed_send))

    @pl.when(section == last)
    def _():
        def owed_left():
            pl.when(my_part == 0)(lambda: wait(owed.at[pl.ds(0, width - 1)], owe_send))
            pl.when(my_part > 0)(lambda: wait(owed, owe_send))

        if_slicing(owed_left)
        for q in range(parts):
            span = partial.at[
                pl.ds(0, width if q else width - 1), :, pl.ds(plan.start[q], plan.size[q])
            ]
            wait(span, part_send.at[q])

    for q in range(parts):
        @pl.when(section == last - q)
        def _():
            for far in range(1, sections):
                wait(done_out.at[:, :, pl.ds(plan.off[q], plan.size[q])], done_send.at[far])


def shards(inputs, router, w_up, w_down, picks, probe):
    sections = lax.axis_size("pipe")
    width = lax.axis_size("expert")
    tokens, features = inputs.shape[1:]
    experts = router.shape[2]
    cap = picks.shape[3]
    hidden_units = w_up.shape[1]
    feats = probe.shape[1]
    piece = features // CUT
    slots = sections * experts
    blocks = -(-slots // BLOCK)
    plan = Plan(sections, width, features)
    window, parts = plan.window, plan.parts
    any_spec = pl.BlockSpec(memory_space=pl.ANY)
    low, wide = jnp.bfloat16, jnp.float32
    state = (slots, cap, window) if sections > 2 else (1, 8, LANE)
    dma = pltpu.SemaphoreType.DMA
    out = pl.pallas_call(
        functools.partial(kernel, sections, width, experts, plan),
        out_shape=jax.ShapeDtypeStruct((tokens, feats), jnp.bfloat16),
        in_specs=[any_spec] * 6,
        out_specs=pl.BlockSpec(memory_space=pltpu.VMEM),
        scratch_shapes=[
            pltpu.VMEM((tokens, features), low),
            pltpu.VMEM((hidden_units + PAD, features), low),
            pltpu.VMEM((hidden_units, features), low),
            pltpu.VMEM((feats, features), low),
            pltpu.VMEM((experts, features), low),
            pltpu.VMEM((sections, experts, cap), jnp.int32),
            pltpu.VMEM((slots, cap, LANE), wide),
            pltpu.VMEM((slots, CUT, LANE), wide),
            pltpu.VMEM((experts, CUT, piece), low),
            pltpu.VMEM((width, CUT, piece), low),
            pltpu.VMEM((piece // LANE, width * CUT, LANE), wide),
            pltpu.VMEM((CUT, cap, piece), low),
            pltpu.VMEM((CUT, blocks, BLOCK, piece), low),
            pltpu.VMEM((width, blocks, BLOCK, window), low),
            pltpu.VMEM((slots, cap, window), wide),
            pltpu.VMEM((width, cap, window), low),
            pltpu.VMEM(state, low),
            pltpu.VMEM(state, low),
            pltpu.VMEM((experts, cap, window), low),
            pltpu.VMEM((width, cap, window), low),
            pltpu.VMEM((width, blocks, BLOCK, window), low),
            pltpu.VMEM((CUT, blocks, BLOCK, window), low),
            pltpu.VMEM((window // LANE, slots * CUT, LANE), wide),
            pltpu.VMEM((width, CUT, piece), low),
            pltpu.VMEM((width, CUT, window), low),
            pltpu.VMEM((slots, CUT, window), low),
            pltpu.VMEM((parts, slots, CUT, window), low),
            dma((6,)), dma((sections,)), dma((sections,)), dma, dma,
            dma, dma, dma, dma, dma, dma,
            dma, dma((width,)), dma, dma,
            dma((parts,)), dma, dma((sections,)), dma((parts,)),
        ],
        compiler_params=pltpu.CompilerParams(collective_id=0, has_side_effects=True),
        name="relay",
    )(inputs[0], jnp.transpose(router[0]), w_up[0], w_down[0], picks[0, 0], probe[0])
    return out[None, None]


def solution(mesh):
    return jax.shard_map(
        shards,
        mesh=mesh,
        in_specs=(
            P(None, "expert", None),
            P("pipe", None, None),
            P("pipe", "expert", None),
            P("pipe", "expert", None),
            P("pipe", None, None, None),
            P("pipe", None, None),
        ),
        out_specs=P("pipe", None, "expert", None),
        check_vma=False,
    )
```

```python
import functools

import jax
import jax.numpy as jnp
from jax import lax
from jax.experimental import pallas as pl
from jax.experimental.pallas import tpu as pltpu
from jax.sharding import PartitionSpec as P

EPS = 1e-06
CUT = 8
PAD = 16
JOIN = 2
GROUPS = 2
GRANT = 24 << 20
LANE = 128
BLOCK = 8
MESH = pl.DeviceIdType.MESH
NT = (((1,), (1,)), ((), ()))


class Plan:
    def __init__(self, sections, width, features):
        self.piece = features // CUT
        tiles = self.piece // LANE
        self.per = width // CUT
        self.parts = min(self.per, tiles, sections)
        sizes = [tiles // self.parts + (q < tiles % self.parts) for q in range(self.parts)]
        starts = [sum(sizes[:q]) for q in range(self.parts)]
        self.window = max(sizes) * LANE
        self.size = [size * LANE for size in sizes]
        self.start = [start * LANE for start in starts]
        self.win = [min(start, self.piece - self.window) for start in self.start]
        self.off = [start - win for start, win in zip(self.start, self.win)]


def kernel(
    sections, width, experts, plan, x_hbm, router_hbm, up_hbm, down_hbm, picks_hbm, probe_hbm,
    out_ref, x_ref, up_ref, down_ref, probe_ref, scorer, lists, columns, place, picked, arrived,
    stage, listed, xrows, xin, base_rows, pin, state_out, state_in, sent, fed, owed, owing, held,
    partial, returned, done_out, done_in, load_sem, list_send, list_recv, row_send, row_recv,
    x_send, x_recv, pin_send, pin_recv, state_send, state_recv, fed_send, fed_recv, owe_send,
    owe_recv, part_send, part_recv, done_send, done_recv, swap_send, swap_recv, self_sem, ready,
):
    section = lax.axis_index("pipe")
    me = lax.axis_index("expert")
    tokens, features = x_ref.shape
    hidden_units = up_hbm.shape[0]
    cap = lists.shape[2]
    piece, per, parts, window = plan.piece, plan.per, plan.parts, plan.window
    group = width // experts
    slots = sections * experts
    blocks, filled = xin.shape[1], min(slots, BLOCK)
    last = sections - 1
    expert = me // group
    my_cut = me // per
    my_part = lax.rem(me, per)
    barrier = pltpu.get_barrier_semaphore()

    def far_pipe(far):
        index = section + far
        return jnp.where(index >= sections, index - sections, index)

    def each_other(act):
        if width <= 16:
            for step in reversed(range(1, width)):
                act(jnp.bitwise_xor(me, step))
        else:
            lax.fori_loop(
                1, width, lambda step, carry: (act(jnp.bitwise_xor(me, width - step)), carry)[1], 0
            )

    def if_slicing(act):
        if per == parts:
            act()
        else:
            pl.when(my_part < parts)(act)

    def remote(src, dst, send, recv, to):
        return pltpu.make_async_remote_copy(
            src_ref=src, dst_ref=dst, send_sem=send, recv_sem=recv, device_id=to,
            device_id_type=MESH,
        )

    def wait(ref, sem):
        pltpu.make_async_copy(ref, ref, sem).wait()

    partners = [jnp.bitwise_xor(me, group * k) for k in range(1, experts)]
    block = [jnp.bitwise_xor(me, m) for m in reversed(range(1, group))]

    def greet(others):
        for other in others:
            pl.semaphore_signal(
                barrier, inc=1, device_id=(section, other), device_id_type=MESH
            )

    greet(partners)
    greet(block)
    for far in range(1, sections):
        pl.semaphore_signal(barrier, inc=1, device_id=(far_pipe(far), me), device_id_type=MESH)

    loads = [
        pltpu.make_async_copy(picks_hbm, lists.at[section], load_sem.at[0]),
        pltpu.make_async_copy(x_hbm, x_ref, load_sem.at[1]),
        pltpu.make_async_copy(up_hbm, up_ref.at[pl.ds(0, hidden_units)], load_sem.at[2]),
        pltpu.make_async_copy(router_hbm, scorer, load_sem.at[3]),
        pltpu.make_async_copy(down_hbm, down_ref, load_sem.at[4]),
        pltpu.make_async_copy(probe_hbm, probe_ref, load_sem.at[5]),
    ]
    for load in loads:
        load.start()
    loads[0].wait()
    loads[1].wait()

    def places_of(section_lists):
        wide = jnp.concatenate(
            [jnp.broadcast_to(section_lists[e : e + 1], (CUT, section_lists.shape[1]))
             for e in range(experts)], axis=0,
        )
        local = wide - me * tokens
        owned = (local >= 0) & (local < tokens)
        found = jnp.where(owned, local + 1, 0).astype(jnp.float32)
        return jnp.sum(found, axis=1, keepdims=True) - 1.0

    def select(places):
        height = experts * CUT
        token_id = lax.broadcasted_iota(jnp.int32, (height, tokens), 1).astype(jnp.float32)
        cut_id = lax.rem(lax.broadcasted_iota(jnp.int32, (height, tokens), 0), CUT)
        hot = places == token_id
        total = jnp.zeros((height, piece), jnp.float32)
        for c in range(CUT):
            pick = jnp.where(hot & (cut_id == c), 1.0, 0.0).astype(jnp.bfloat16)
            total += jnp.dot(
                pick, x_ref[:, c * piece : (c + 1) * piece], preferred_element_type=jnp.float32
            )
        return total

    def note(which):
        section_lists = lists[which]
        places = places_of(section_lists)
        place[pl.ds(which * experts, experts)] = jnp.broadcast_to(
            places, (experts * CUT, LANE)
        ).reshape(experts, CUT, LANE)
        diagonal = lax.broadcasted_iota(jnp.int32, (cap, cap), 0) == lax.broadcasted_iota(
            jnp.int32, (cap, cap), 1
        )
        for e in range(experts):
            wide = jnp.broadcast_to(section_lists[e : e + 1], (cap, cap)).astype(jnp.float32)
            column = jnp.sum(jnp.where(diagonal, wide, 0.0), axis=1, keepdims=True)
            columns[which * experts + e] = jnp.broadcast_to(column, columns.shape[1:])
        return places

    places = note(section)

    @pl.when(section == 0)
    def _():
        picked[...] = select(places).astype(jnp.bfloat16).reshape(experts, CUT, piece)

    pl.semaphore_wait(barrier, group - 1 + experts - 1 + sections - 1)

    def expert_of(index):
        owner = jnp.int32(0)
        for e in range(1, experts):
            owner = owner + (index >= e * group).astype(jnp.int32)
        return owner

    @pl.when(section == 0)
    def _():
        for k in range(1, experts):
            remote(
                picked.at[jnp.bitwise_xor(expert, k)], arrived.at[me], swap_send, swap_recv.at[k],
                (section, partners[k - 1]),
            ).start()
        for other in block:
            remote(
                picked.at[expert], arrived.at[me], row_send, row_recv, (section, other)
            ).start()
        pltpu.make_async_copy(picked.at[expert], arrived.at[me], self_sem).start()

    for other in partners:
        pl.semaphore_signal(ready.at[0], inc=1, device_id=(section, other), device_id_type=MESH)

    def list_copy(far):
        return remote(
            lists.at[section], lists.at[section], list_send.at[far], list_recv.at[far],
            (far_pipe(far), me),
        )

    for far in range(1, sections):
        list_copy(far).start()

    loads[5].wait()
    x_all = x_ref[...]
    raw = lax.dot_general(x_all, probe_ref[...], NT, preferred_element_type=jnp.float32)
    x_wide = x_all.astype(jnp.float32)
    square = jnp.sum(x_wide * x_wide, axis=1, keepdims=True)
    base = raw * lax.rsqrt(square * (1.0 / features) + EPS)

    @pl.when(section == 0)
    def _():
        for k in range(1, experts):
            wait(arrived.at[partners[k - 1]], swap_recv.at[k])
        for other in block:
            for partner in partners:
                remote(
                    arrived.at[partner], arrived.at[partner], row_send, row_recv, (section, other)
                ).start()

    pl.semaphore_wait(ready.at[0], experts - 1)
    for far in range(1, sections):
        pl.semaphore_signal(
            ready.at[1], inc=1, device_id=(far_pipe(far), me), device_id_type=MESH
        )
    for far in range(1, sections):
        list_copy(far).wait()
        note(lax.rem(section + sections - far, sections))

    def each_slice(act):
        for step in reversed(range(CUT)):
            cut = jnp.bitwise_xor(my_cut, step)
            for q in range(parts):
                act(step, cut, q, cut * per + q)

    def owner_lanes(height_rows, first_block):
        rows_n, lanes_n = filled * cap, width * BLOCK
        row_slot = lax.broadcasted_iota(jnp.int32, (rows_n, lanes_n), 0) // cap
        lane = lax.broadcasted_iota(jnp.int32, (rows_n, lanes_n), 1)
        low = (lane // BLOCK * tokens).astype(jnp.float32)
        return (row_slot == lane % BLOCK) & (height_rows >= low) & (height_rows < low + tokens)

    def column_of(block):
        wide = columns[pl.ds(block * filled, filled)]
        return wide.reshape(filled * cap, wide.shape[2])[:, :1]

    def row_of(column):
        count = column.shape[0]
        diagonal = lax.broadcasted_iota(jnp.int32, (count, count), 0) == lax.broadcasted_iota(
            jnp.int32, (count, count), 1
        )
        wide = jnp.where(diagonal, jnp.broadcast_to(column, (count, count)), 0.0)
        return jnp.sum(wide, axis=0, keepdims=True)

    @pl.when(section == 1)
    def _():
        token_id = lax.broadcasted_iota(jnp.int32, (BLOCK, tokens), 1).astype(jnp.float32)
        row_id = lax.broadcasted_iota(jnp.int32, (BLOCK, tokens), 0)
        for b in range(blocks):
            hot = jnp.zeros((BLOCK, tokens), jnp.float32)
            for i in range(filled):
                at = place[b * filled + i][:1, :1]
                hot = jnp.where((row_id == i) & (at == token_id), 1.0, hot)
            for c in range(CUT):
                xrows[c, b] = jnp.dot(
                    hot.astype(jnp.bfloat16), x_ref[:, c * piece : (c + 1) * piece],
                    preferred_element_type=jnp.float32,
                ).astype(jnp.bfloat16)

        def send(step, cut, q, device):
            src = xrows.at[cut, :, :, pl.ds(plan.win[q], window)]

            def away():
                remote(src, xin.at[me], x_send, x_recv, (section, device)).start()

            if step:
                away()
            else:
                pl.when(device != me)(away)

                @pl.when(device == me)
                def _():
                    pltpu.make_async_copy(src, xin.at[me], x_recv).start()

        each_slice(send)

    loads[2].wait()
    loads[3].wait()
    up_ref[pl.ds(hidden_units, PAD)] = jnp.zeros((PAD, features), jnp.bfloat16)
    up_ref[pl.ds(hidden_units, experts)] = scorer[...]
    loads[4].wait()
    pl.semaphore_wait(ready.at[1], sections - 1)

    @pl.when(section == 1)
    def _():
        def gather():
            wait(xin, x_recv)
            for b in range(blocks):
                rows = xin[:, b].astype(jnp.float32).reshape(width * BLOCK, window)
                hot = owner_lanes(column_of(b), b).astype(jnp.float32).astype(jnp.bfloat16)
                total = jnp.dot(hot, rows.astype(jnp.bfloat16), preferred_element_type=jnp.float32)
                base_rows[pl.ds(b * filled, filled)] = total.reshape(filled, cap, window)

        if_slicing(gather)

    def hidden_of(pre, squares):
        scale = lax.rsqrt(squares * (1.0 / features) + EPS)
        pre = pre * scale
        column = lax.broadcasted_iota(jnp.int32, pre.shape, 1)
        logit = jnp.sum(
            jnp.where(column == hidden_units + expert, pre, 0.0), axis=1, keepdims=True
        )
        value = pre[:, :hidden_units]
        gate = 1.0 / (1.0 + jnp.exp(-logit))
        return (value / (1.0 + jnp.exp(-value)) * gate).astype(jnp.bfloat16)

    def first_hidden():
        wait(arrived.at[me], self_sem)
        wait(arrived.at[pl.ds(0, (group - 1) * experts)], row_recv)
        wide = arrived[...].astype(jnp.float32).reshape(width * CUT, piece)
        for t in range(piece // LANE):
            stage[t] = wide[:, t * LANE : (t + 1) * LANE]
        squares = jnp.sum((wide * wide).reshape(width, CUT, piece), axis=1)
        pre = jnp.zeros((width, up_ref.shape[0]), jnp.float32)
        for c in range(0, CUT, JOIN):
            pre += lax.dot_general(
                jnp.concatenate(
                    [stage[t, pl.ds(c + i, width, stride=CUT)]
                     for i in range(JOIN) for t in range(piece // LANE)], axis=1
                ).astype(jnp.bfloat16),
                up_ref[:, c * piece : (c + JOIN) * piece], NT,
                preferred_element_type=jnp.float32,
            )
        hidden = hidden_of(pre, jnp.sum(squares, axis=1, keepdims=True))
        column = columns[section * experts + expert][:, :1]
        low = (lax.broadcasted_iota(jnp.int32, (cap, width), 1) * tokens).astype(jnp.float32)
        hot = jnp.where((column >= low) & (column < low + tokens), 1.0, 0.0).astype(jnp.bfloat16)
        return jnp.dot(hot, hidden, preferred_element_type=jnp.float32).astype(jnp.bfloat16)

    def next_hidden():
        pre = jnp.zeros((cap, up_ref.shape[0]), jnp.float32)
        squares = jnp.zeros((cap, 1), jnp.float32)
        span = CUT // GROUPS
        for first in range(0, CUT, span):
            start = jnp.bitwise_xor(my_cut // span * span, first)
            for i in range(span):
                for q in range(parts):
                    device = (start + i) * per + q
                    wait(fed.at[device], fed_recv.at[device])
            chunk = jnp.concatenate(
                [fed[(start + i) * per + q][:, plan.off[q] : plan.off[q] + plan.size[q]]
                 for i in range(span) for q in range(parts)], axis=1,
            )
            wide = chunk.astype(jnp.float32)
            squares += jnp.sum(wide * wide, axis=1, keepdims=True)
            pre += lax.dot_general(
                chunk, up_ref[:, pl.ds(pl.multiple_of(start * piece, LANE), span * piece)], NT,
                preferred_element_type=jnp.float32,
            )
        return hidden_of(pre, squares)

    def pass_lists(hidden):
        for c in range(0, CUT, JOIN):
            block = jnp.dot(
                hidden, down_ref[:, c * piece : (c + JOIN) * piece],
                preferred_element_type=jnp.float32,
            ).astype(jnp.bfloat16)
            for i in range(JOIN):
                listed[c + i] = block[:, i * piece : (i + 1) * piece]

        def send(step, cut, q, device):
            remote(
                listed.at[cut, :, pl.ds(plan.win[q], window)], pin.at[me], pin_send, pin_recv,
                (section + 1, device),
            ).start()

        each_slice(send)

    def share_parts(hidden):
        own_list = jnp.zeros((1, cap), jnp.int32)
        for e in range(experts):
            own_list = jnp.where(expert == e, lists[section][e : e + 1], own_list)
        low = lax.broadcasted_iota(jnp.int32, (width, cap), 0) * tokens
        hot = (own_list >= low) & (own_list < low + tokens)
        hidden = jnp.dot(
            jnp.where(hot, 1.0, 0.0).astype(jnp.bfloat16), hidden,
            preferred_element_type=jnp.float32,
        ).astype(jnp.bfloat16)
        for c in range(0, CUT, JOIN):
            block = jnp.dot(
                hidden, down_ref[:, c * piece : (c + JOIN) * piece],
                preferred_element_type=jnp.float32,
            )
            for i in range(JOIN):
                for t in range(piece // LANE):
                    at = i * piece + t * LANE
                    stage[t, pl.ds(c + i, width, stride=CUT)] = block[:, at : at + LANE]
        for t in range(piece // LANE):
            partial[:, :, t * LANE : (t + 1) * LANE] = (
                stage[t].reshape(width, CUT, LANE).astype(jnp.bfloat16)
            )

        def refs(owner, q):
            return (
                partial.at[owner, :, pl.ds(plan.start[q], plan.size[q])],
                returned.at[me, :, pl.ds(plan.off[q], plan.size[q])],
            )

        def give(owner, q):
            src, dst = refs(owner, q)
            remote(src, dst, part_send.at[q], part_recv, (section - q, owner)).start()

        for q in reversed(range(1, parts)):
            give(me, q)

        def give_all(owner):
            for q in reversed(range(parts)):
                give(owner, q)

        each_other(give_all)
        src, dst = refs(me, 0)
        pltpu.make_async_copy(src, dst, part_recv).start()

    def state_copy():
        return remote(state_out, state_in, state_send, state_recv, (section + 1, me))

    def take_lists(last_section):
        if sections > 2:
            @pl.when(section > 1)
            def _():
                wait(state_in, state_recv)
                base_rows[...] = state_in[...].astype(jnp.float32)

        before = columns[pl.ds((section - 1) * experts, experts)]
        entries = row_of(before.reshape(experts * cap, before.shape[2])[:, :1])

        def matches(first, count):
            wide = columns[pl.ds(first, count)]
            same = wide.reshape(count * cap, wide.shape[2])[:, :1] == entries
            return jnp.where(same, 1.0, 0.0).astype(jnp.bfloat16)

        own = matches(section * experts, experts)
        wait(pin, pin_recv)
        sums = jnp.concatenate(
            [jnp.sum(pin[pl.ds(e * group, group)].astype(jnp.float32), axis=0)
             for e in range(experts)], axis=0,
        )
        high = sums.astype(jnp.bfloat16)
        low = (sums - high.astype(jnp.float32)).astype(jnp.bfloat16)

        def grow(hot, first, count):
            added = jnp.dot(hot, high, preferred_element_type=jnp.float32) + jnp.dot(
                hot, low, preferred_element_type=jnp.float32
            )
            rows = base_rows[pl.ds(first, count)] + added.reshape(count, cap, window)
            return rows.astype(jnp.bfloat16)

        sent[...] = grow(own, section * experts, experts)
        each_other(
            lambda other: remote(
                sent.at[expert_of(other)], fed.at[me], fed_send, fed_recv.at[me], (section, other)
            ).start()
        )
        pltpu.make_async_copy(sent.at[expert], fed.at[me], fed_recv.at[me]).start()
        for b in range(blocks):
            rows = grow(matches(b * filled, filled), b * filled, filled)
            if sections > 2:
                state_out[pl.ds(b * filled, filled)] = rows
            owed_block(b, rows.reshape(filled * cap, window))
        if sections > 2:
            pl.when(section < last)(lambda: state_copy().start())
        pl.when(section == last)(owe)

    def owed_block(b, rows):
        @pl.when(section == last)
        def _():
            rows_n, lanes_n = width * BLOCK, filled * cap
            entry = row_of(column_of(b))
            row = lax.broadcasted_iota(jnp.int32, (rows_n, lanes_n), 0)
            lane_slot = lax.broadcasted_iota(jnp.int32, (rows_n, lanes_n), 1) // cap
            low = (row // BLOCK * tokens).astype(jnp.float32)
            hot = (row % BLOCK == lane_slot) & (entry >= low) & (entry < low + tokens)
            total = jnp.dot(
                jnp.where(hot, 1.0, 0.0).astype(jnp.bfloat16), rows,
                preferred_element_type=jnp.float32,
            )
            owed[:, b] = total.reshape(width, BLOCK, window).astype(jnp.bfloat16)

    def owe():
        def send(owner):
            remote(
                owed.at[owner], owing.at[my_cut], owe_send, owe_recv, (last - my_part, owner)
            ).start()

        each_other(send)
        pl.when(my_part > 0)(lambda: send(me))

        @pl.when(my_part == 0)
        def _():
            pltpu.make_async_copy(owed.at[me], owing.at[my_cut], owe_recv).start()

    @pl.when(section == 0)
    def _():
        pass_lists(first_hidden())

    if sections > 2:
        @pl.when((section > 0) & (section < last))
        def _():
            if_slicing(lambda: take_lists(False))
            pass_lists(next_hidden())

    @pl.when(section == last)
    def _():
        if_slicing(lambda: take_lists(True))
        share_parts(next_hidden())

    def done_copy(far):
        mine = last - section
        return remote(
            done_out, done_in.at[mine], done_send.at[far], done_recv.at[mine],
            (far_pipe(far), me),
        )

    def finish(q):
        wait(owing, owe_recv)
        for c in range(CUT):
            for b in range(blocks):
                rows = owing[c, b].astype(jnp.float32)
                for t in range(window // LANE):
                    held[t, pl.ds(b * filled * CUT + c, filled, stride=CUT)] = rows[
                        :filled, t * LANE : (t + 1) * LANE
                    ]
        span = returned.at[:, :, pl.ds(plan.off[q], plan.size[q])]
        wait(span, part_recv)
        lanes = slice(plan.off[q], plan.off[q] + plan.size[q])
        updates = [
            jnp.sum(returned[pl.ds(e * group, group), :, lanes].astype(jnp.float32), axis=0)
            for e in range(experts)
        ]
        for slot in range(slots):
            for t in range(plan.size[q] // LANE):
                tile = plan.off[q] // LANE + t
                rows = held[tile, pl.ds(slot * CUT, CUT)]
                for e in range(experts):
                    same = place[slot] == place[last * experts + e]
                    rows += jnp.where(same, updates[e][:, t * LANE : (t + 1) * LANE], 0.0)
                done_out[slot, :, tile * LANE : (tile + 1) * LANE] = rows.astype(jnp.bfloat16)
        for far in range(1, sections):
            remote(
                done_out.at[:, :, pl.ds(plan.off[q], plan.size[q])],
                done_in.at[q, :, :, pl.ds(plan.off[q], plan.size[q])],
                done_send.at[far], done_recv.at[q], (far_pipe(far), me),
            ).start()

        done_in[q, :, :, lanes] = done_out[:, :, lanes]

    for q in range(parts):
        pl.when(section == last - q)(functools.partial(finish, q))

    for q in range(parts):
        @pl.when(section != last - q)
        def _():
            wait(done_in.at[q, :, :, pl.ds(plan.off[q], plan.size[q])], done_recv.at[q])

    def over_cuts(value):
        count, lanes = value.shape
        summed = jnp.sum(value.reshape(count // CUT, CUT, lanes), axis=1, keepdims=True)
        return jnp.broadcast_to(summed, (count // CUT, CUT, lanes)).reshape(count, lanes)

    height = slots * CUT
    wide = jnp.concatenate(
        [done_in[q][:, :, plan.off[q] : plan.off[q] + plan.size[q]].astype(jnp.float32)
         for q in range(parts)], axis=2,
    ).reshape(height, piece)
    mean = over_cuts(jnp.sum(wide * wide, axis=1, keepdims=True)) * (1.0 / features)
    narrow = wide.astype(jnp.bfloat16)
    feats = probe_ref.shape[0]
    cut_out = lax.rem(lax.broadcasted_iota(jnp.int32, (height, feats), 0), CUT)
    changed = jnp.zeros((height, feats), jnp.float32)
    for c in range(CUT):
        term = lax.dot_general(
            narrow, probe_ref[:, c * piece : (c + 1) * piece], NT,
            preferred_element_type=jnp.float32,
        )
        changed = jnp.where(cut_out == c, term, changed)
    changed = over_cuts(changed) * lax.rsqrt(mean + EPS)
    token_id = lax.broadcasted_iota(jnp.int32, (tokens, feats), 0).astype(jnp.float32)
    result = base
    for slot in range(slots):
        at = place[slot][:1, :feats]
        result = jnp.where(token_id == at, changed[slot * CUT : slot * CUT + 1], result)
    out_ref[...] = result.astype(out_ref.dtype)

    @pl.when(section == 0)
    def _():
        wait(arrived.at[pl.ds(0, (group - 1) * experts)], row_send)
        wait(picked.at[pl.ds(0, experts - 1)], swap_send)

    @pl.when(section < last)
    def _():
        for _ in range(1):
            whole = pin.at[pl.ds(0, CUT * parts)]
            wait(whole, pin_send)
        if sections > 2:
            @pl.when(section > 0)
            def _():
                if_slicing(lambda: wait(state_out, state_send))

    @pl.when(section == 1)
    def _():
        slices = CUT * parts
        if per == parts:
            wait(xin.at[pl.ds(0, slices - 1)], x_send)
        else:
            pl.when(my_part < parts)(lambda: wait(xin.at[pl.ds(0, slices - 1)], x_send))
            pl.when(my_part >= parts)(lambda: wait(xin.at[pl.ds(0, slices)], x_send))

    @pl.when(section > 0)
    def _():
        if_slicing(lambda: wait(fed.at[pl.ds(0, width - 1)], fed_send))

    @pl.when(section == last)
    def _():
        def owed_left():
            pl.when(my_part == 0)(lambda: wait(owed.at[pl.ds(0, width - 1)], owe_send))
            pl.when(my_part > 0)(lambda: wait(owed, owe_send))

        if_slicing(owed_left)
        for q in range(parts):
            span = partial.at[
                pl.ds(0, width if q else width - 1), :, pl.ds(plan.start[q], plan.size[q])
            ]
            wait(span, part_send.at[q])

    for q in range(parts):
        @pl.when(section == last - q)
        def _():
            for far in range(1, sections):
                wait(done_out.at[:, :, pl.ds(plan.off[q], plan.size[q])], done_send.at[far])


def shards(inputs, router, w_up, w_down, picks, probe):
    sections = lax.axis_size("pipe")
    width = lax.axis_size("expert")
    tokens, features = inputs.shape[1:]
    experts = router.shape[2]
    cap = picks.shape[3]
    hidden_units = w_up.shape[1]
    feats = probe.shape[1]
    piece = features // CUT
    slots = sections * experts
    blocks = -(-slots // BLOCK)
    plan = Plan(sections, width, features)
    window, parts = plan.window, plan.parts
    any_spec = pl.BlockSpec(memory_space=pl.ANY)
    low, wide = jnp.bfloat16, jnp.float32
    state = (slots, cap, window) if sections > 2 else (1, 8, LANE)
    dma = pltpu.SemaphoreType.DMA
    arrays = (
        inputs[0], jnp.transpose(router[0]), w_up[0], w_down[0], picks[0, 0], probe[0],
    )
    out = pl.pallas_call(
        functools.partial(kernel, sections, width, experts, plan),
        out_shape=jax.ShapeDtypeStruct((tokens, feats), jnp.bfloat16),
        in_specs=[any_spec] * 6,
        out_specs=pl.BlockSpec(memory_space=pltpu.VMEM),
        scratch_shapes=[
            pltpu.VMEM((tokens, features), low),
            pltpu.VMEM((hidden_units + PAD, features), low),
            pltpu.VMEM((hidden_units, features), low),
            pltpu.VMEM((feats, features), low),
            pltpu.VMEM((experts, features), low),
            pltpu.VMEM((sections, experts, cap), jnp.int32),
            pltpu.VMEM((slots, cap, LANE), wide),
            pltpu.VMEM((slots, CUT, LANE), wide),
            pltpu.VMEM((experts, CUT, piece), low),
            pltpu.VMEM((width, CUT, piece), low),
            pltpu.VMEM((piece // LANE, width * CUT, LANE), wide),
            pltpu.VMEM((CUT, cap, piece), low),
            pltpu.VMEM((CUT, blocks, BLOCK, piece), low),
            pltpu.VMEM((width, blocks, BLOCK, window), low),
            pltpu.VMEM((slots, cap, window), wide),
            pltpu.VMEM((width, cap, window), low),
            pltpu.VMEM(state, low),
            pltpu.VMEM(state, low),
            pltpu.VMEM((experts, cap, window), low),
            pltpu.VMEM((width, cap, window), low),
            pltpu.VMEM((width, blocks, BLOCK, window), low),
            pltpu.VMEM((CUT, blocks, BLOCK, window), low),
            pltpu.VMEM((window // LANE, slots * CUT, LANE), wide),
            pltpu.VMEM((width, CUT, piece), low),
            pltpu.VMEM((width, CUT, window), low),
            pltpu.VMEM((slots, CUT, window), low),
            pltpu.VMEM((parts, slots, CUT, window), low),
            dma((6,)), dma((sections,)), dma((sections,)), dma, dma,
            dma, dma, dma, dma, dma, dma,
            dma, dma((width,)), dma, dma,
            dma((parts,)), dma, dma((sections,)), dma((parts,)),
            dma, dma((experts,)), dma, pltpu.SemaphoreType.REGULAR((2,)),
        ],
        compiler_params=pltpu.CompilerParams(
            collective_id=0, has_side_effects=True, vmem_limit_bytes=GRANT
        ),
        name="relay",
    )(*[pltpu.with_memory_space_constraint(array, pltpu.HBM) for array in arrays])
    return out[None, None]


def solution(mesh):
    return jax.shard_map(
        shards,
        mesh=mesh,
        in_specs=(
            P(None, "expert", None),
            P("pipe", None, None),
            P("pipe", "expert", None),
            P("pipe", "expert", None),
            P("pipe", None, None, None),
            P("pipe", None, None),
        ),
        out_specs=P("pipe", None, "expert", None),
        check_vma=False,
    )
```

```python
import functools

import jax
import jax.numpy as jnp
from jax import lax
from jax.experimental import pallas as pl
from jax.experimental.pallas import tpu as pltpu
from jax.sharding import PartitionSpec as P

EPS = 1e-06
CUT = 8
PAD = 16
JOIN = 2
GROUPS = 2
GRANT = 24 << 20
LANE = 128
BLOCK = 8
MESH = pl.DeviceIdType.MESH
NT = (((1,), (1,)), ((), ()))


class Plan:
    def __init__(self, sections, width, features):
        self.piece = features // CUT
        tiles = self.piece // LANE
        self.per = width // CUT
        self.parts = min(self.per, tiles, sections)
        sizes = [tiles // self.parts + (q < tiles % self.parts) for q in range(self.parts)]
        starts = [sum(sizes[:q]) for q in range(self.parts)]
        self.window = max(sizes) * LANE
        self.size = [size * LANE for size in sizes]
        self.start = [start * LANE for start in starts]
        self.win = [min(start, self.piece - self.window) for start in self.start]
        self.off = [start - win for start, win in zip(self.start, self.win)]


def kernel(
    sections, width, experts, plan, x_hbm, router_hbm, up_hbm, down_hbm, picks_hbm, probe_hbm,
    out_ref, x_ref, up_ref, down_ref, probe_ref, scorer, lists, columns, place, picked, arrived,
    stage, listed, xrows, xin, base_rows, pin, state_out, state_in, sent, fed, owed, owing, held,
    partial, returned, done_out, done_in, load_sem, list_send, list_recv, row_send, row_recv,
    x_send, x_recv, pin_send, pin_recv, state_send, state_recv, fed_send, fed_recv, owe_send,
    owe_recv, part_send, part_recv, done_send, done_recv, swap_send, swap_recv, self_sem, ready,
):
    section = lax.axis_index("pipe")
    me = lax.axis_index("expert")
    tokens, features = x_ref.shape
    hidden_units = up_hbm.shape[0]
    cap = lists.shape[2]
    piece, per, parts, window = plan.piece, plan.per, plan.parts, plan.window
    group = width // experts
    slots = sections * experts
    blocks, filled = xin.shape[1], min(slots, BLOCK)
    last = sections - 1
    expert = me // group
    my_cut = me // per
    my_part = lax.rem(me, per)
    barrier = pltpu.get_barrier_semaphore()

    def far_pipe(far):
        index = section + far
        return jnp.where(index >= sections, index - sections, index)

    def each_other(act):
        if width <= 16:
            for step in reversed(range(1, width)):
                act(jnp.bitwise_xor(me, step))
        else:
            lax.fori_loop(
                1, width, lambda step, carry: (act(jnp.bitwise_xor(me, width - step)), carry)[1], 0
            )

    def if_slicing(act):
        if per == parts:
            act()
        else:
            pl.when(my_part < parts)(act)

    def remote(src, dst, send, recv, to):
        return pltpu.make_async_remote_copy(
            src_ref=src, dst_ref=dst, send_sem=send, recv_sem=recv, device_id=to,
            device_id_type=MESH,
        )

    def wait(ref, sem):
        pltpu.make_async_copy(ref, ref, sem).wait()

    partners = [jnp.bitwise_xor(me, group * k) for k in range(1, experts)]
    block = [jnp.bitwise_xor(me, m) for m in reversed(range(1, group))]

    def greet(others):
        for other in others:
            pl.semaphore_signal(
                barrier, inc=1, device_id=(section, other), device_id_type=MESH
            )

    greet(partners)
    greet(block)
    for far in range(1, sections):
        pl.semaphore_signal(barrier, inc=1, device_id=(far_pipe(far), me), device_id_type=MESH)

    loads = [
        pltpu.make_async_copy(picks_hbm, lists.at[section], load_sem.at[0]),
        pltpu.make_async_copy(x_hbm, x_ref, load_sem.at[1]),
        pltpu.make_async_copy(up_hbm, up_ref.at[pl.ds(0, hidden_units)], load_sem.at[2]),
        pltpu.make_async_copy(router_hbm, scorer, load_sem.at[3]),
        pltpu.make_async_copy(down_hbm, down_ref, load_sem.at[4]),
        pltpu.make_async_copy(probe_hbm, probe_ref, load_sem.at[5]),
    ]
    for load in loads:
        load.start()
    loads[0].wait()
    loads[1].wait()

    def places_of(section_lists):
        wide = jnp.concatenate(
            [jnp.broadcast_to(section_lists[e : e + 1], (CUT, section_lists.shape[1]))
             for e in range(experts)], axis=0,
        )
        local = wide - me * tokens
        owned = (local >= 0) & (local < tokens)
        found = jnp.where(owned, local + 1, 0).astype(jnp.float32)
        return jnp.sum(found, axis=1, keepdims=True) - 1.0

    def select(places):
        height = experts * CUT
        token_id = lax.broadcasted_iota(jnp.int32, (height, tokens), 1).astype(jnp.float32)
        cut_id = lax.rem(lax.broadcasted_iota(jnp.int32, (height, tokens), 0), CUT)
        hot = places == token_id
        total = jnp.zeros((height, piece), jnp.float32)
        for c in range(CUT):
            pick = jnp.where(hot & (cut_id == c), 1.0, 0.0).astype(jnp.bfloat16)
            total += jnp.dot(
                pick, x_ref[:, c * piece : (c + 1) * piece], preferred_element_type=jnp.float32
            )
        return total

    def note(which):
        section_lists = lists[which]
        places = places_of(section_lists)
        place[pl.ds(which * experts, experts)] = jnp.broadcast_to(
            places, (experts * CUT, LANE)
        ).reshape(experts, CUT, LANE)
        diagonal = lax.broadcasted_iota(jnp.int32, (cap, cap), 0) == lax.broadcasted_iota(
            jnp.int32, (cap, cap), 1
        )
        for e in range(experts):
            wide = jnp.broadcast_to(section_lists[e : e + 1], (cap, cap)).astype(jnp.float32)
            column = jnp.sum(jnp.where(diagonal, wide, 0.0), axis=1, keepdims=True)
            columns[which * experts + e] = jnp.broadcast_to(column, columns.shape[1:])
        return places

    places = note(section)

    @pl.when(section == 0)
    def _():
        picked[...] = select(places).astype(jnp.bfloat16).reshape(experts, CUT, piece)

    pl.semaphore_wait(barrier, group - 1 + experts - 1 + sections - 1)

    def expert_of(index):
        owner = jnp.int32(0)
        for e in range(1, experts):
            owner = owner + (index >= e * group).astype(jnp.int32)
        return owner

    @pl.when(section == 0)
    def _():
        for k in range(1, experts):
            remote(
                picked.at[jnp.bitwise_xor(expert, k)], arrived.at[me], swap_send, swap_recv.at[k],
                (section, partners[k - 1]),
            ).start()
        for other in block:
            remote(
                picked.at[expert], arrived.at[me], row_send, row_recv, (section, other)
            ).start()
        pltpu.make_async_copy(picked.at[expert], arrived.at[me], self_sem).start()

    for other in partners:
        pl.semaphore_signal(ready.at[0], inc=1, device_id=(section, other), device_id_type=MESH)

    def list_copy(far):
        return remote(
            lists.at[section], lists.at[section], list_send.at[far], list_recv.at[far],
            (far_pipe(far), me),
        )

    for far in range(1, sections):
        list_copy(far).start()

    loads[5].wait()
    x_all = x_ref[...]
    raw = lax.dot_general(x_all, probe_ref[...], NT, preferred_element_type=jnp.float32)
    x_wide = x_all.astype(jnp.float32)
    square = jnp.sum(x_wide * x_wide, axis=1, keepdims=True)
    base = raw * lax.rsqrt(square * (1.0 / features) + EPS)

    @pl.when(section == 0)
    def _():
        for k in range(1, experts):
            wait(arrived.at[partners[k - 1]], swap_recv.at[k])
        for other in block:
            for partner in partners:
                remote(
                    arrived.at[partner], arrived.at[partner], row_send, row_recv, (section, other)
                ).start()

    pl.semaphore_wait(ready.at[0], experts - 1)
    for far in range(1, sections):
        pl.semaphore_signal(
            ready.at[1], inc=1, device_id=(far_pipe(far), me), device_id_type=MESH
        )
    for far in range(1, sections):
        list_copy(far).wait()
        note(lax.rem(section + sections - far, sections))

    def each_slice(act):
        for step in reversed(range(CUT)):
            cut = jnp.bitwise_xor(my_cut, step)
            for q in range(parts):
                act(step, cut, q, cut * per + q)

    def owner_lanes(height_rows, first_block):
        rows_n, lanes_n = filled * cap, width * BLOCK
        row_slot = lax.broadcasted_iota(jnp.int32, (rows_n, lanes_n), 0) // cap
        lane = lax.broadcasted_iota(jnp.int32, (rows_n, lanes_n), 1)
        low = (lane // BLOCK * tokens).astype(jnp.float32)
        return (row_slot == lane % BLOCK) & (height_rows >= low) & (height_rows < low + tokens)

    def column_of(block):
        wide = columns[pl.ds(block * filled, filled)]
        return wide.reshape(filled * cap, wide.shape[2])[:, :1]

    def row_of(column):
        count = column.shape[0]
        diagonal = lax.broadcasted_iota(jnp.int32, (count, count), 0) == lax.broadcasted_iota(
            jnp.int32, (count, count), 1
        )
        wide = jnp.where(diagonal, jnp.broadcast_to(column, (count, count)), 0.0)
        return jnp.sum(wide, axis=0, keepdims=True)

    @pl.when(section == 1)
    def _():
        token_id = lax.broadcasted_iota(jnp.int32, (BLOCK, tokens), 1).astype(jnp.float32)
        row_id = lax.broadcasted_iota(jnp.int32, (BLOCK, tokens), 0)
        for b in range(blocks):
            hot = jnp.zeros((BLOCK, tokens), jnp.float32)
            for i in range(filled):
                at = place[b * filled + i][:1, :1]
                hot = jnp.where((row_id == i) & (at == token_id), 1.0, hot)
            for c in range(CUT):
                xrows[c, b] = jnp.dot(
                    hot.astype(jnp.bfloat16), x_ref[:, c * piece : (c + 1) * piece],
                    preferred_element_type=jnp.float32,
                ).astype(jnp.bfloat16)

        def send(step, cut, q, device):
            src = xrows.at[cut, :, :, pl.ds(plan.win[q], window)]

            def away():
                remote(src, xin.at[me], x_send, x_recv, (section, device)).start()

            if step:
                away()
            else:
                pl.when(device != me)(away)

                @pl.when(device == me)
                def _():
                    pltpu.make_async_copy(src, xin.at[me], x_recv).start()

        each_slice(send)

    loads[2].wait()
    loads[3].wait()
    up_ref[pl.ds(hidden_units, PAD)] = jnp.zeros((PAD, features), jnp.bfloat16)
    up_ref[pl.ds(hidden_units, experts)] = scorer[...]
    loads[4].wait()
    pl.semaphore_wait(ready.at[1], sections - 1)

    @pl.when(section == 1)
    def _():
        def gather():
            wait(xin, x_recv)
            for b in range(blocks):
                rows = xin[:, b].astype(jnp.float32).reshape(width * BLOCK, window)
                hot = owner_lanes(column_of(b), b).astype(jnp.float32).astype(jnp.bfloat16)
                total = jnp.dot(hot, rows.astype(jnp.bfloat16), preferred_element_type=jnp.float32)
                base_rows[pl.ds(b * filled, filled)] = total.reshape(filled, cap, window)

        if_slicing(gather)

    def hidden_of(pre, squares):
        scale = lax.rsqrt(squares * (1.0 / features) + EPS)
        pre = pre * scale
        column = lax.broadcasted_iota(jnp.int32, pre.shape, 1)
        logit = jnp.sum(
            jnp.where(column == hidden_units + expert, pre, 0.0), axis=1, keepdims=True
        )
        value = pre[:, :hidden_units]
        gate = 1.0 / (1.0 + jnp.exp(-logit))
        return (value / (1.0 + jnp.exp(-value)) * gate).astype(jnp.bfloat16)

    def first_hidden():
        wait(arrived.at[me], self_sem)
        wait(arrived.at[pl.ds(0, (group - 1) * experts)], row_recv)
        wide = arrived[...].astype(jnp.float32).reshape(width * CUT, piece)
        for t in range(piece // LANE):
            stage[t] = wide[:, t * LANE : (t + 1) * LANE]
        squares = jnp.sum((wide * wide).reshape(width, CUT, piece), axis=1)
        pre = jnp.zeros((width, up_ref.shape[0]), jnp.float32)
        for c in range(0, CUT, JOIN):
            pre += lax.dot_general(
                jnp.concatenate(
                    [stage[t, pl.ds(c + i, width, stride=CUT)]
                     for i in range(JOIN) for t in range(piece // LANE)], axis=1
                ).astype(jnp.bfloat16),
                up_ref[:, c * piece : (c + JOIN) * piece], NT,
                preferred_element_type=jnp.float32,
            )
        hidden = hidden_of(pre, jnp.sum(squares, axis=1, keepdims=True))
        column = columns[section * experts + expert][:, :1]
        low = (lax.broadcasted_iota(jnp.int32, (cap, width), 1) * tokens).astype(jnp.float32)
        hot = jnp.where((column >= low) & (column < low + tokens), 1.0, 0.0).astype(jnp.bfloat16)
        return jnp.dot(hot, hidden, preferred_element_type=jnp.float32).astype(jnp.bfloat16)

    def next_hidden():
        pre = jnp.zeros((cap, up_ref.shape[0]), jnp.float32)
        squares = jnp.zeros((cap, 1), jnp.float32)
        span = CUT // GROUPS
        for first in range(0, CUT, span):
            start = jnp.bitwise_xor(my_cut // span * span, first)
            for i in range(span):
                for q in range(parts):
                    device = (start + i) * per + q
                    wait(fed.at[device], fed_recv.at[device])
            if first == 0:
                pl.when(section == last)(lambda: if_slicing(owe))
            chunk = jnp.concatenate(
                [fed[(start + i) * per + q][:, plan.off[q] : plan.off[q] + plan.size[q]]
                 for i in range(span) for q in range(parts)], axis=1,
            )
            wide = chunk.astype(jnp.float32)
            squares += jnp.sum(wide * wide, axis=1, keepdims=True)
            pre += lax.dot_general(
                chunk, up_ref[:, pl.ds(pl.multiple_of(start * piece, LANE), span * piece)], NT,
                preferred_element_type=jnp.float32,
            )
        return hidden_of(pre, squares)

    def pass_lists(hidden):
        span = CUT // GROUPS

        def send(step, cut, q, device):
            if step % span == span - 1 and q == 0:
                first = cut // span * span
                block = jnp.dot(
                    hidden,
                    down_ref[:, pl.ds(pl.multiple_of(first * piece, LANE), span * piece)],
                    preferred_element_type=jnp.float32,
                ).astype(jnp.bfloat16)
                for i in range(span):
                    listed[first + i] = block[:, i * piece : (i + 1) * piece]
            remote(
                listed.at[cut, :, pl.ds(plan.win[q], window)], pin.at[me], pin_send, pin_recv,
                (section + 1, device),
            ).start()

        each_slice(send)

    def share_parts(hidden):
        own_list = jnp.zeros((1, cap), jnp.int32)
        for e in range(experts):
            own_list = jnp.where(expert == e, lists[section][e : e + 1], own_list)
        low = lax.broadcasted_iota(jnp.int32, (width, cap), 0) * tokens
        hot = (own_list >= low) & (own_list < low + tokens)
        hidden = jnp.dot(
            jnp.where(hot, 1.0, 0.0).astype(jnp.bfloat16), hidden,
            preferred_element_type=jnp.float32,
        ).astype(jnp.bfloat16)
        def refs(owner, q):
            return (
                partial.at[owner, :, pl.ds(plan.start[q], plan.size[q])],
                returned.at[me, :, pl.ds(plan.off[q], plan.size[q])],
            )

        def give(owner, q):
            src, dst = refs(owner, q)
            remote(src, dst, part_send.at[q], part_recv, (section - q, owner)).start()

        for q in reversed(range(parts)):
            first, count, size = plan.start[q] // LANE, plan.size[q] // LANE, plan.size[q]
            for c in range(0, CUT, JOIN):
                columns_of = [
                    down_ref[:, pl.ds((c + i) * piece + plan.start[q], size)] for i in range(JOIN)
                ]
                product = jnp.dot(
                    hidden, jnp.concatenate(columns_of, axis=1),
                    preferred_element_type=jnp.float32,
                )
                for i in range(JOIN):
                    for t in range(count):
                        at = i * size + t * LANE
                        stage[first + t, pl.ds(c + i, width, stride=CUT)] = product[
                            :, at : at + LANE
                        ]
            for t in range(first, first + count):
                partial[:, :, t * LANE : (t + 1) * LANE] = (
                    stage[t].reshape(width, CUT, LANE).astype(jnp.bfloat16)
                )
            each_other(functools.partial(give, q=q))
            if q:
                give(me, q)
        src, dst = refs(me, 0)
        pltpu.make_async_copy(src, dst, part_recv).start()

    def state_copy():
        return remote(state_out, state_in, state_send, state_recv, (section + 1, me))

    def take_lists(last_section):
        if sections > 2:
            @pl.when(section > 1)
            def _():
                wait(state_in, state_recv)
                base_rows[...] = state_in[...].astype(jnp.float32)

        before = columns[pl.ds((section - 1) * experts, experts)]
        entries = row_of(before.reshape(experts * cap, before.shape[2])[:, :1])

        def matches(first, count):
            wide = columns[pl.ds(first, count)]
            same = wide.reshape(count * cap, wide.shape[2])[:, :1] == entries
            return jnp.where(same, 1.0, 0.0).astype(jnp.bfloat16)

        own = matches(section * experts, experts)
        wait(pin, pin_recv)
        sums = jnp.concatenate(
            [jnp.sum(pin[pl.ds(e * group, group)].astype(jnp.float32), axis=0)
             for e in range(experts)], axis=0,
        )
        high = sums.astype(jnp.bfloat16)
        low = (sums - high.astype(jnp.float32)).astype(jnp.bfloat16)

        def grow(hot, first, count):
            added = jnp.dot(hot, high, preferred_element_type=jnp.float32) + jnp.dot(
                hot, low, preferred_element_type=jnp.float32
            )
            rows = base_rows[pl.ds(first, count)] + added.reshape(count, cap, window)
            return rows.astype(jnp.bfloat16)

        sent[...] = grow(own, section * experts, experts)
        each_other(
            lambda other: remote(
                sent.at[expert_of(other)], fed.at[me], fed_send, fed_recv.at[me], (section, other)
            ).start()
        )
        pltpu.make_async_copy(sent.at[expert], fed.at[me], fed_recv.at[me]).start()
        for b in range(blocks):
            rows = grow(matches(b * filled, filled), b * filled, filled)
            if sections > 2:
                state_out[pl.ds(b * filled, filled)] = rows
            owed_block(b, rows.reshape(filled * cap, window))
        if sections > 2:
            pl.when(section < last)(lambda: state_copy().start())

    def owed_block(b, rows):
        @pl.when(section == last)
        def _():
            rows_n, lanes_n = width * BLOCK, filled * cap
            entry = row_of(column_of(b))
            row = lax.broadcasted_iota(jnp.int32, (rows_n, lanes_n), 0)
            lane_slot = lax.broadcasted_iota(jnp.int32, (rows_n, lanes_n), 1) // cap
            low = (row // BLOCK * tokens).astype(jnp.float32)
            hot = (row % BLOCK == lane_slot) & (entry >= low) & (entry < low + tokens)
            total = jnp.dot(
                jnp.where(hot, 1.0, 0.0).astype(jnp.bfloat16), rows,
                preferred_element_type=jnp.float32,
            )
            owed[:, b] = total.reshape(width, BLOCK, window).astype(jnp.bfloat16)

    def owe():
        def send(owner):
            remote(
                owed.at[owner], owing.at[my_cut], owe_send, owe_recv, (last - my_part, owner)
            ).start()

        each_other(send)
        pl.when(my_part > 0)(lambda: send(me))

        @pl.when(my_part == 0)
        def _():
            pltpu.make_async_copy(owed.at[me], owing.at[my_cut], owe_recv).start()

    @pl.when(section == 0)
    def _():
        pass_lists(first_hidden())

    if sections > 2:
        @pl.when((section > 0) & (section < last))
        def _():
            if_slicing(lambda: take_lists(False))
            pass_lists(next_hidden())

    @pl.when(section == last)
    def _():
        if_slicing(lambda: take_lists(True))
        share_parts(next_hidden())

    def done_copy(far):
        mine = last - section
        return remote(
            done_out, done_in.at[mine], done_send.at[far], done_recv.at[mine],
            (far_pipe(far), me),
        )

    def finish(q):
        wait(owing, owe_recv)
        for c in range(CUT):
            for b in range(blocks):
                rows = owing[c, b].astype(jnp.float32)
                for t in range(window // LANE):
                    held[t, pl.ds(b * filled * CUT + c, filled, stride=CUT)] = rows[
                        :filled, t * LANE : (t + 1) * LANE
                    ]
        span = returned.at[:, :, pl.ds(plan.off[q], plan.size[q])]
        wait(span, part_recv)
        lanes = slice(plan.off[q], plan.off[q] + plan.size[q])
        updates = [
            jnp.sum(returned[pl.ds(e * group, group), :, lanes].astype(jnp.float32), axis=0)
            for e in range(experts)
        ]
        for slot in range(slots):
            for t in range(plan.size[q] // LANE):
                tile = plan.off[q] // LANE + t
                rows = held[tile, pl.ds(slot * CUT, CUT)]
                for e in range(experts):
                    same = place[slot] == place[last * experts + e]
                    rows += jnp.where(same, updates[e][:, t * LANE : (t + 1) * LANE], 0.0)
                done_out[slot, :, tile * LANE : (tile + 1) * LANE] = rows.astype(jnp.bfloat16)
        for far in range(1, sections):
            remote(
                done_out.at[:, :, pl.ds(plan.off[q], plan.size[q])],
                done_in.at[q, :, :, pl.ds(plan.off[q], plan.size[q])],
                done_send.at[far], done_recv.at[q], (far_pipe(far), me),
            ).start()

        done_in[q, :, :, lanes] = done_out[:, :, lanes]

    for q in range(parts):
        pl.when(section == last - q)(functools.partial(finish, q))

    for q in range(parts):
        @pl.when(section != last - q)
        def _():
            wait(done_in.at[q, :, :, pl.ds(plan.off[q], plan.size[q])], done_recv.at[q])

    def over_cuts(value):
        count, lanes = value.shape
        summed = jnp.sum(value.reshape(count // CUT, CUT, lanes), axis=1, keepdims=True)
        return jnp.broadcast_to(summed, (count // CUT, CUT, lanes)).reshape(count, lanes)

    height = slots * CUT
    wide = jnp.concatenate(
        [done_in[q][:, :, plan.off[q] : plan.off[q] + plan.size[q]].astype(jnp.float32)
         for q in range(parts)], axis=2,
    ).reshape(height, piece)
    mean = over_cuts(jnp.sum(wide * wide, axis=1, keepdims=True)) * (1.0 / features)
    narrow = wide.astype(jnp.bfloat16)
    feats = probe_ref.shape[0]
    cut_out = lax.rem(lax.broadcasted_iota(jnp.int32, (height, feats), 0), CUT)
    changed = jnp.zeros((height, feats), jnp.float32)
    for c in range(CUT):
        term = lax.dot_general(
            narrow, probe_ref[:, c * piece : (c + 1) * piece], NT,
            preferred_element_type=jnp.float32,
        )
        changed = jnp.where(cut_out == c, term, changed)
    changed = over_cuts(changed) * lax.rsqrt(mean + EPS)
    token_id = lax.broadcasted_iota(jnp.int32, (tokens, feats), 0).astype(jnp.float32)
    result = base
    for slot in range(slots):
        at = place[slot][:1, :feats]
        result = jnp.where(token_id == at, changed[slot * CUT : slot * CUT + 1], result)
    out_ref[...] = result.astype(out_ref.dtype)

    @pl.when(section == 0)
    def _():
        wait(arrived.at[pl.ds(0, (group - 1) * experts)], row_send)
        wait(picked.at[pl.ds(0, experts - 1)], swap_send)

    @pl.when(section < last)
    def _():
        for _ in range(1):
            whole = pin.at[pl.ds(0, CUT * parts)]
            wait(whole, pin_send)
        if sections > 2:
            @pl.when(section > 0)
            def _():
                if_slicing(lambda: wait(state_out, state_send))

    @pl.when(section == 1)
    def _():
        slices = CUT * parts
        if per == parts:
            wait(xin.at[pl.ds(0, slices - 1)], x_send)
        else:
            pl.when(my_part < parts)(lambda: wait(xin.at[pl.ds(0, slices - 1)], x_send))
            pl.when(my_part >= parts)(lambda: wait(xin.at[pl.ds(0, slices)], x_send))

    @pl.when(section > 0)
    def _():
        if_slicing(lambda: wait(fed.at[pl.ds(0, width - 1)], fed_send))

    @pl.when(section == last)
    def _():
        def owed_left():
            pl.when(my_part == 0)(lambda: wait(owed.at[pl.ds(0, width - 1)], owe_send))
            pl.when(my_part > 0)(lambda: wait(owed, owe_send))

        if_slicing(owed_left)
        for q in range(parts):
            span = partial.at[
                pl.ds(0, width if q else width - 1), :, pl.ds(plan.start[q], plan.size[q])
            ]
            wait(span, part_send.at[q])

    for q in range(parts):
        @pl.when(section == last - q)
        def _():
            for far in range(1, sections):
                wait(done_out.at[:, :, pl.ds(plan.off[q], plan.size[q])], done_send.at[far])


def shards(inputs, router, w_up, w_down, picks, probe):
    sections = lax.axis_size("pipe")
    width = lax.axis_size("expert")
    tokens, features = inputs.shape[1:]
    experts = router.shape[2]
    cap = picks.shape[3]
    hidden_units = w_up.shape[1]
    feats = probe.shape[1]
    piece = features // CUT
    slots = sections * experts
    blocks = -(-slots // BLOCK)
    plan = Plan(sections, width, features)
    window, parts = plan.window, plan.parts
    any_spec = pl.BlockSpec(memory_space=pl.ANY)
    low, wide = jnp.bfloat16, jnp.float32
    state = (slots, cap, window) if sections > 2 else (1, 8, LANE)
    dma = pltpu.SemaphoreType.DMA
    arrays = (
        inputs[0], jnp.transpose(router[0]), w_up[0], w_down[0], picks[0, 0], probe[0],
    )
    out = pl.pallas_call(
        functools.partial(kernel, sections, width, experts, plan),
        out_shape=jax.ShapeDtypeStruct((tokens, feats), jnp.bfloat16),
        in_specs=[any_spec] * 6,
        out_specs=pl.BlockSpec(memory_space=pltpu.VMEM),
        scratch_shapes=[
            pltpu.VMEM((tokens, features), low),
            pltpu.VMEM((hidden_units + PAD, features), low),
            pltpu.VMEM((hidden_units, features), low),
            pltpu.VMEM((feats, features), low),
            pltpu.VMEM((experts, features), low),
            pltpu.VMEM((sections, experts, cap), jnp.int32),
            pltpu.VMEM((slots, cap, LANE), wide),
            pltpu.VMEM((slots, CUT, LANE), wide),
            pltpu.VMEM((experts, CUT, piece), low),
            pltpu.VMEM((width, CUT, piece), low),
            pltpu.VMEM((piece // LANE, width * CUT, LANE), wide),
            pltpu.VMEM((CUT, cap, piece), low),
            pltpu.VMEM((CUT, blocks, BLOCK, piece), low),
            pltpu.VMEM((width, blocks, BLOCK, window), low),
            pltpu.VMEM((slots, cap, window), wide),
            pltpu.VMEM((width, cap, window), low),
            pltpu.VMEM(state, low),
            pltpu.VMEM(state, low),
            pltpu.VMEM((experts, cap, window), low),
            pltpu.VMEM((width, cap, window), low),
            pltpu.VMEM((width, blocks, BLOCK, window), low),
            pltpu.VMEM((CUT, blocks, BLOCK, window), low),
            pltpu.VMEM((window // LANE, slots * CUT, LANE), wide),
            pltpu.VMEM((width, CUT, piece), low),
            pltpu.VMEM((width, CUT, window), low),
            pltpu.VMEM((slots, CUT, window), low),
            pltpu.VMEM((parts, slots, CUT, window), low),
            dma((6,)), dma((sections,)), dma((sections,)), dma, dma,
            dma, dma, dma, dma, dma, dma,
            dma, dma((width,)), dma, dma,
            dma((parts,)), dma, dma((sections,)), dma((parts,)),
            dma, dma((experts,)), dma, pltpu.SemaphoreType.REGULAR((2,)),
        ],
        compiler_params=pltpu.CompilerParams(
            collective_id=0, has_side_effects=True, vmem_limit_bytes=GRANT
        ),
        name="relay",
    )(*[pltpu.with_memory_space_constraint(array, pltpu.HBM) for array in arrays])
    return out[None, None]


def solution(mesh):
    return jax.shard_map(
        shards,
        mesh=mesh,
        in_specs=(
            P(None, "expert", None),
            P("pipe", None, None),
            P("pipe", "expert", None),
            P("pipe", "expert", None),
            P("pipe", None, None, None),
            P("pipe", None, None),
        ),
        out_specs=P("pipe", None, "expert", None),
        check_vma=False,
    )
```
